32 devices in a mesh: rows: 16 (over z, y, x), cols: 2 (over core).
Axes of the slice: x: 2, y: 2, z: 4, core: 2. Of those that a mesh axis runs over, the one named last changes fastest.
Arguments:
- iterate: bfloat16 [24576, 512], P('rows', 'cols'), may hold values from -256 to 256, as said below
- residual: bfloat16 [24576, 512], P('rows', 'cols'), may hold values from -256 to 256, as said below
- leaf_offset: bfloat16 [24576, 768], P('rows', 'cols'), may hold values from -0.109375 to 0.109375
- bases_v: bfloat16 [5, 24576, 256], P(None, 'rows', 'cols'), may hold values from -1 to 1, as said below
- bases_u: bfloat16 [5, 24576, 256], P(None, 'rows', 'cols'), may hold values from -0.1875 to 0.1875
- estimate: float32 [512], P('cols'), may hold values from -1 to 1
Outputs:
- updated: float32 [24576, 512], P('rows', 'cols')
- functional: float32 [512], P('cols')
The draws below stay inside these ranges and needn't reach their ends.
Inputs may be any that keep to these rules, and one draw needn't show every extreme that they name: Entries of the iterate, real valued. Entries of the residual, real valued. `bases_v`: real valued basis entries.
All inputs are finite; a program needn't handle non-finite values.
Results may differ from the reference program's by a relative error of at most 0.0085.
Values may be sent and summed in bfloat16 or wider, within the bound.
A program may use at most 64 MiB of HBM per device.

```python
import jax
import jax.numpy as jnp
from jax import lax

R = 256
VECS = 512
ROWS = 1536
LEAF = 768
LEVELS = 4
TREE = 5
TOTAL = 24576


def shared_parts(key):
    keys = jax.random.split(jax.random.fold_in(key, 29), 5)
    block_count = TOTAL // ROWS
    roughness = 10.0 ** (0.6 * jax.random.uniform(keys[0], (block_count, ROWS, 1), dtype=jnp.float32) - 0.3)
    column_scale = 2.0 ** (2.0 * jax.random.uniform(keys[1], (1, 1, VECS), dtype=jnp.float32) - 1.0)
    amplitude = 10.0 ** (1.5 * jax.random.uniform(keys[2], (block_count, 1, VECS), dtype=jnp.float32) - 0.75)
    coupling = jax.random.uniform(keys[3], (block_count, 1, VECS), dtype=jnp.float32, minval=-1.0, maxval=1.0)
    common_field = jnp.clip(jax.random.normal(keys[4], (block_count, ROWS, VECS), dtype=jnp.float32), -3.5, 3.5)
    return (common_field, coupling, roughness * amplitude * column_scale)


def private_field(key, salt):
    keys = jax.random.split(jax.random.fold_in(key, salt), 1)
    block_count = TOTAL // ROWS
    return jnp.clip(jax.random.normal(keys[0], (block_count, ROWS, VECS), dtype=jnp.float32), -3.5, 3.5)


def draw_iterate(key, part):
    common_field, coupling, scale = shared_parts(key)
    values = (private_field(key, 11) + common_field) * scale
    return values.reshape(TOTAL, VECS).astype(jnp.bfloat16)


def draw_residual(key, part):
    common_field, coupling, scale = shared_parts(key)
    values = (private_field(key, 17) + 2.0 * coupling * common_field) * scale
    return values.reshape(TOTAL, VECS).astype(jnp.bfloat16)


def draw_bases_v(key, part):
    basis_key = jax.random.fold_in(key, 23)
    depth = jnp.arange(TREE, dtype=jnp.float32)
    level_scale = jnp.sqrt(2.0 ** depth / TOTAL)[:, None, None]
    values = jnp.clip(jax.random.normal(basis_key, (TREE, TOTAL, R), dtype=jnp.float32), -4.0, 4.0)
    return (values * level_scale).astype(jnp.bfloat16)


def shard_levels(rng, dims, shards, smallest, top_value):
    def one(position, blocks):
        heights = jax.random.uniform(jax.random.fold_in(jax.random.fold_in(rng, 6), position), (blocks,), jnp.float32, smallest / len(shards), top_value / len(shards))
        return jnp.repeat(jnp.exp(heights), dims[position] // blocks).reshape((-1,) + (1,) * (len(dims) - position - 1))

    factor_of = one(*shards[0])
    for cut in shards[1:]:
        factor_of = factor_of * one(*cut)
    return factor_of


def centred(own_key, extent, deviation, most, cuts=(), kind=jnp.bfloat16):
    values = jax.random.normal(own_key, extent, jnp.float32) * deviation
    if len(cuts) > 0:
        values = shard_levels(own_key, extent, cuts, -0.22, 0.18) * values
    return jnp.clip(values, min=-most, max=most).astype(kind)


def setup_inputs(seed: int = 0) -> dict:
    key_of = jax.random.split(jax.random.key(seed), 7)
    iterate = draw_iterate(jax.random.fold_in(key_of[6], 71), 0)
    residual = draw_residual(jax.random.fold_in(key_of[6], 71), 0)
    leaf_offset = centred(key_of[2], (TOTAL, LEAF), (4 * LEAF) ** -0.5, 0.109375, ((0, 16), (1, 2)))
    bases_v = draw_bases_v(jax.random.fold_in(key_of[6], 71), 0)
    bases_u = centred(key_of[4], (TREE, TOTAL, R), (4 * R) ** -0.5, 0.1875, ((1, 16), (2, 2)))
    estimate = jnp.clip(jax.random.uniform(key_of[5], (VECS,), jnp.float32, -1.0, 1.0) * shard_levels(key_of[5], (VECS,), ((0, 2),), -0.4, 0.0), -1.0, 1.0)
    return {"iterate": iterate, "residual": residual, "leaf_offset": leaf_offset, "bases_v": bases_v, "bases_u": bases_u, "estimate": estimate}


epsilon = 1e-6


def leaf_product(paired):
    return jnp.dot(paired[0], paired[1], preferred_element_type=jnp.float32)


def project_node(paired):
    return lax.dot_general(paired[0], paired[1], (((0,), (0,)), ((), ())), preferred_element_type=jnp.float32)


def reference(iterate, residual, leaf_offset, bases_v, bases_u, estimate):
    leaf_count = TOTAL // LEAF
    residual_blocks = residual.reshape(leaf_count, LEAF, VECS)
    offset_blocks = leaf_offset.reshape(leaf_count, LEAF, LEAF)
    leaf_terms = lax.map(leaf_product, (offset_blocks, residual_blocks))
    current = residual.astype(jnp.float32) + leaf_terms.reshape(TOTAL, VECS)
    for level_index in range(LEVELS, -1, -1):
        node_count = 2 ** level_index
        node_rows = TOTAL // node_count
        rounded = current.astype(jnp.bfloat16).reshape(node_count, node_rows, VECS)
        right_nodes = bases_v[level_index].reshape(node_count, node_rows, R)
        coefficients = lax.map(project_node, (right_nodes, rounded))
        narrow = coefficients.astype(jnp.bfloat16)
        left_nodes = bases_u[level_index].reshape(node_count, node_rows, R)
        correction = lax.map(leaf_product, (left_nodes, narrow))
        current = current - correction.reshape(TOTAL, VECS)
    updated = iterate.astype(jnp.float32) - current
    numerator = jnp.sum(updated * residual.astype(jnp.float32), axis=0)
    denominator = jnp.sum(updated * updated, axis=0)
    functional = estimate + numerator / (denominator + epsilon)
    return updated, functional
```

```python
import functools

import jax
import jax.numpy as jnp
from jax import lax
from jax.experimental import pallas as pl
from jax.experimental.pallas import tpu as pltpu
from jax.sharding import PartitionSpec as P

epsilon = 1e-06
MESH = pl.DeviceIdType.MESH
MOST = 16


def log2(value):
    return value.bit_length() - 1


def tdot(a, b):
    return lax.dot_general(a, b, (((0,), (0,)), ((), ())), preferred_element_type=jnp.float32)


def dot(a, b):
    return jnp.dot(a, b, preferred_element_type=jnp.float32)


def kernel(n, it_h, r_h, leaf_h, v_h, u_h, est_ref, out_h, fun_ref,
           it, r, rp, leaf, v, u, x, pf, ps, rs, c, xs, xr, st, sg, sx,
           lsem, wsend, wrecv, ssem, rsem, xsem, osem):
    rows, vecs = r.shape
    rank = v.shape[2]
    half = rank // 2
    width = leaf.shape[1]
    lh = width // 2
    top = log2(n)
    most = min(n, MOST)
    me = lax.axis_index("rows")
    col = lax.axis_index("cols")
    other = 1 - col

    local = []

    def fetch(src, dst, slot):
        copy = pltpu.make_async_copy(src, dst, lsem.at[slot])
        copy.start()
        return copy

    base = 0
    got_r = []
    for k in range(rows // width):
        for part, which in enumerate((col, other)):
            start = pl.multiple_of(k * width + which * lh, 16)
            got_r.append(fetch(r_h.at[pl.ds(start, lh)], rp.at[pl.ds(k * width + part * lh, lh)], base))
            base += 1
    got_r.append(fetch(r_h, r, base))
    got_leaf = fetch(leaf_h, leaf.at[:, pl.ds(0, lh)], base + 1)
    base += 2
    got_v, got_u = {}, {}
    for l in range(top, -1, -1):
        got_v[l] = fetch(v_h.at[l], v.at[l, :, pl.ds(0, half)], base)
        got_u[l] = fetch(u_h.at[l], u.at[l, :, pl.ds(0, half)], base + 1)
        base += 2
    got_it = fetch(it_h, it, base)

    barrier = pltpu.get_barrier_semaphore()
    pl.semaphore_signal(barrier, inc=1, device_id={"cols": other}, device_id_type=MESH)
    peers = list(range(1, most)) + [most << b for b in range(log2(n // most))]
    for o in peers:
        pl.semaphore_signal(barrier, inc=1, device_id={"rows": me ^ o}, device_id_type=MESH)
    pl.semaphore_wait(barrier, len(peers) + 1)

    sends = []

    def push(src, dst, slot):
        copy = pltpu.make_async_remote_copy(
            src_ref=src, dst_ref=dst, send_sem=wsend.at[slot], recv_sem=wrecv.at[slot],
            device_id={"cols": other}, device_id_type=MESH)
        copy.start()
        sends.append(copy)
        return copy

    in_leaf = push(leaf_h, leaf.at[:, pl.ds(lh, lh)], 0)
    in_v, in_u = {}, {}
    for l in range(top, -1, -1):
        in_v[l] = push(v_h.at[l], v.at[l, :, pl.ds(half, half)], 1 + 2 * l)
        in_u[l] = push(u_h.at[l], u.at[l, :, pl.ds(half, half)], 2 + 2 * l)

    def ready_v(l):
        got_v[l].wait()
        in_v[l].wait_recv()

    def ready_u(l):
        got_u[l].wait()
        in_u[l].wait_recv()

    def send(src, dst, l, phase, o):
        copy = pltpu.make_async_remote_copy(
            src_ref=src, dst_ref=dst, send_sem=ssem.at[l, phase, o], recv_sem=rsem.at[l, phase, o],
            device_id={"rows": me ^ o}, device_id_type=MESH)
        copy.start()
        sends.append(copy)
        return copy

    def send_far(src, dst, l, b):
        copy = pltpu.make_async_remote_copy(
            src_ref=src, dst_ref=dst, send_sem=xsem.at[0, l, b], recv_sem=xsem.at[1, l, b],
            device_id={"rows": me ^ (most << b)}, device_id_type=MESH)
        copy.start()
        sends.append(copy)
        copy.wait_recv()

    for copy in got_r:
        copy.wait()
    got_leaf.wait()
    in_leaf.wait_recv()
    for k in range(rows // width):
        s = pl.ds(k * width, width)
        x[s] = r[s].astype(jnp.float32) + dot(leaf[s], rp[s])
    ready_v(top)
    narrow = tdot(v[top], x[...].astype(jnp.bfloat16)).astype(jnp.bfloat16)
    ready_u(top)
    x[...] = x[...] - dot(u[top], narrow)
    ready_v(top - 1)
    partial = tdot(v[top - 1], x[...].astype(jnp.bfloat16))

    for l in range(top - 1, -1, -1):
        group = 2 ** (top - l)
        h = min(group, most)
        pair = h == 2
        ch = rank if pair else rank // h
        j = me & (h - 1)
        mine = pl.ds(pl.multiple_of(j * ch, 16), ch)
        ps[l] = partial.astype(jnp.bfloat16)
        if pair:
            moved = [send(ps.at[l], rs.at[l], l, 0, 1)]
        else:
            moved = [
                send(ps.at[l, pl.ds(pl.multiple_of((j ^ o) * ch, 16), ch)],
                     rs.at[l, pl.ds((o - 1) * ch, ch)], l, 0, o)
                for o in range(h - 1, 0, -1)
            ]
            pf[...] = partial
        if l < top - 1:
            moved_x = x[...] - dot(u[l + 1], c[l + 1])
            x[...] = it[...].astype(jnp.float32) - moved_x if l == 0 else moved_x
        ready_u(l)
        if l == 1:
            got_it.wait()

        def ahead():
            ready_v(l - 1)
            term = tdot(v[l - 1], x[...].astype(jnp.bfloat16))
            cross = tdot(v[l - 1], u[l]).astype(jnp.bfloat16)
            return term, cross

        if pair:
            term, cross = ahead() if l > 0 else (None, None)
            for copy in moved:
                copy.wait_recv()
            c[l] = (partial + rs[l].astype(jnp.float32)).astype(jnp.bfloat16)
        else:
            for copy in moved:
                copy.wait_recv()
            total = pf[mine]
            for o in range(1, h):
                total = total + rs[l, pl.ds((o - 1) * ch, ch)].astype(jnp.float32)
            for b in range(log2(group // h)):
                xs[l, b] = total
                send_far(xs.at[l, b], xr.at[l, b], l, b)
                total = total + xr[l, b]
            c[l, mine] = total.astype(jnp.bfloat16)
            moved = [send(c.at[l, mine], c.at[l, mine], l, 1, o) for o in range(h - 1, 0, -1)]
            term, cross = ahead() if l > 0 else (None, None)
            for copy in moved:
                copy.wait_recv()
        if l > 0:
            partial = term - dot(cross, c[l])

    blocks = 4
    size = rows // blocks
    num = jnp.zeros((1, vecs), jnp.float32)
    den = jnp.zeros((1, vecs), jnp.float32)
    outs = []
    for k in range(blocks):
        s = pl.ds(k * size, size)
        updated = x[s] + dot(u[0, s], c[0])
        x[s] = updated
        copy = pltpu.make_async_copy(x.at[s], out_h.at[s], osem.at[k])
        copy.start()
        outs.append(copy)
        num = num + jnp.sum(updated * r[s].astype(jnp.float32), axis=0, keepdims=True)
        den = den + jnp.sum(updated * updated, axis=0, keepdims=True)
    st[pl.ds(0, 1)] = num
    st[pl.ds(1, 1)] = den
    moved = [send(st, sg.at[o - 1], top, 0, o) for o in range(most - 1, 0, -1)]
    for copy in moved:
        copy.wait_recv()
    total = st[...]
    for o in range(1, most):
        total = total + sg[o - 1]
    for b in range(log2(n // most)):
        sx[b] = total
        send_far(sx.at[b], sx.at[log2(n // most) + b], top, b)
        total = total + sx[log2(n // most) + b]
    fun_ref[...] = est_ref[...] + total[0:1] / (total[1:2] + epsilon)
    for copy in sends:
        copy.wait_send()
    for copy in outs:
        copy.wait()


def per_device(n, iterate, residual, leaf_offset, bases_v, bases_u, estimate):
    rows, vecs = residual.shape
    levels = bases_v.shape[0]
    rank = 2 * bases_v.shape[2]
    width = 2 * leaf_offset.shape[1]
    top = levels - 1
    most = min(n, MOST)
    far = max(log2(n // most), 1)
    hbm = pl.BlockSpec(memory_space=pl.ANY)
    vmem = pl.BlockSpec(memory_space=pltpu.VMEM)
    bf, f32 = jnp.bfloat16, jnp.float32
    updated, functional = pl.pallas_call(
        functools.partial(kernel, n),
        out_shape=(
            jax.ShapeDtypeStruct((rows, vecs), f32),
            jax.ShapeDtypeStruct((1, vecs), f32),
        ),
        in_specs=[hbm] * 5 + [vmem],
        out_specs=(hbm, vmem),
        scratch_shapes=[
            pltpu.VMEM((rows, vecs), bf),
            pltpu.VMEM((rows, vecs), bf),
            pltpu.VMEM((rows, vecs), bf),
            pltpu.VMEM((rows, width), bf),
            pltpu.VMEM((levels, rows, rank), bf),
            pltpu.VMEM((levels, rows, rank), bf),
            pltpu.VMEM((rows, vecs), f32),
            pltpu.VMEM((rank, vecs), f32),
            pltpu.VMEM((top, rank, vecs), bf),
            pltpu.VMEM((top, rank, vecs), bf),
            pltpu.VMEM((top, rank, vecs), bf),
            pltpu.VMEM((top, far, rank // most, vecs), f32),
            pltpu.VMEM((top, far, rank // most, vecs), f32),
            pltpu.VMEM((8, vecs), f32),
            pltpu.VMEM((most, 8, vecs), f32),
            pltpu.VMEM((2 * far, 8, vecs), f32),
            pltpu.SemaphoreType.DMA((2 * (rows // width) + 2 * levels + 3,)),
            pltpu.SemaphoreType.DMA((2 * levels + 1,)),
            pltpu.SemaphoreType.DMA((2 * levels + 1,)),
            pltpu.SemaphoreType.DMA((levels, 2, most)),
            pltpu.SemaphoreType.DMA((levels, 2, most)),
            pltpu.SemaphoreType.DMA((2, levels, far)),
            pltpu.SemaphoreType.DMA((4,)),
        ],
        compiler_params=pltpu.CompilerParams(
            collective_id=0, has_side_effects=True, vmem_limit_bytes=56 << 20
        ),
    )(iterate, residual, leaf_offset, bases_v, bases_u, estimate.reshape(1, vecs))
    return updated, functional.reshape(vecs)


def solution(mesh):
    return jax.shard_map(
        functools.partial(per_device, mesh.shape["rows"]),
        mesh=mesh,
        in_specs=(
            P("rows", "cols"),
            P("rows", "cols"),
            P("rows", "cols"),
            P(None, "rows", "cols"),
            P(None, "rows", "cols"),
            P("cols"),
        ),
        out_specs=(P("rows", "cols"), P("cols")),
        check_vma=False,
    )
```

```python
import functools

import jax
import jax.numpy as jnp
from jax import lax
from jax.experimental import pallas as pl
from jax.experimental.pallas import tpu as pltpu
from jax.sharding import PartitionSpec as P

epsilon = 1e-06
MESH = pl.DeviceIdType.MESH
MOST = 8


def log2(value):
    return value.bit_length() - 1


def tdot(a, b):
    return lax.dot_general(a, b, (((0,), (0,)), ((), ())), preferred_element_type=jnp.float32)


def dot(a, b):
    return jnp.dot(a, b, preferred_element_type=jnp.float32)


def kernel(n, it_h, r_h, leaf_h, v_h, u_h, est_ref, out_h, fun_ref,
           it, r, rp, leaf, v, u, x, pf, ps, rs, c, xs, xr, st, sg, sx,
           lsem, wsend, wrecv, ssem, rsem, xsem, osem):
    rows, vecs = r.shape
    rank = v.shape[2]
    half = rank // 2
    width = leaf.shape[1]
    lh = width // 2
    top = log2(n)
    most = min(n, MOST)
    me = lax.axis_index("rows")
    col = lax.axis_index("cols")
    other = 1 - col

    local = []

    def fetch(src, dst, slot):
        copy = pltpu.make_async_copy(src, dst, lsem.at[slot])
        copy.start()
        return copy

    base = 0
    got_r = []
    for k in range(rows // width):
        for part, which in enumerate((col, other)):
            start = pl.multiple_of(k * width + which * lh, 16)
            got_r.append(fetch(r_h.at[pl.ds(start, lh)], rp.at[pl.ds(k * width + part * lh, lh)], base))
            base += 1
    got_r.append(fetch(r_h, r, base))
    got_leaf = fetch(leaf_h, leaf.at[:, pl.ds(0, lh)], base + 1)
    base += 2
    got_v, got_u = {}, {}
    for l in range(top, -1, -1):
        got_v[l] = fetch(v_h.at[l], v.at[l, :, pl.ds(0, half)], base)
        got_u[l] = fetch(u_h.at[l], u.at[l, :, pl.ds(0, half)], base + 1)
        base += 2
    got_it = fetch(it_h, it, base)

    barrier = pltpu.get_barrier_semaphore()
    pl.semaphore_signal(barrier, inc=1, device_id={"cols": other}, device_id_type=MESH)
    peers = list(range(1, most)) + [most << b for b in range(log2(n // most))]
    for o in peers:
        pl.semaphore_signal(barrier, inc=1, device_id={"rows": me ^ o}, device_id_type=MESH)
    pl.semaphore_wait(barrier, len(peers) + 1)

    sends = []

    def push(src, dst, slot):
        copy = pltpu.make_async_remote_copy(
            src_ref=src, dst_ref=dst, send_sem=wsend.at[slot], recv_sem=wrecv.at[slot],
            device_id={"cols": other}, device_id_type=MESH)
        copy.start()
        sends.append(copy)
        return copy

    in_leaf = push(leaf_h, leaf.at[:, pl.ds(lh, lh)], 0)
    in_v, in_u = {}, {}

    def push_v(l):
        in_v[l] = push(v_h.at[l], v.at[l, :, pl.ds(half, half)], 1 + 2 * l)

    def push_u(l):
        in_u[l] = push(u_h.at[l], u.at[l, :, pl.ds(half, half)], 2 + 2 * l)

    push_v(top)
    push_u(top)
    push_v(top - 1)
    push_u(top - 1)
    push_v(top - 2)

    def ready_v(l):
        got_v[l].wait()
        in_v[l].wait_recv()

    def ready_u(l):
        got_u[l].wait()
        in_u[l].wait_recv()

    def send(src, dst, l, phase, o):
        copy = pltpu.make_async_remote_copy(
            src_ref=src, dst_ref=dst, send_sem=ssem.at[l, phase, o], recv_sem=rsem.at[l, phase, o],
            device_id={"rows": me ^ o}, device_id_type=MESH)
        copy.start()
        sends.append(copy)
        return copy

    def send_far(src, dst, l, b):
        copy = pltpu.make_async_remote_copy(
            src_ref=src, dst_ref=dst, send_sem=xsem.at[0, l, b], recv_sem=xsem.at[1, l, b],
            device_id={"rows": me ^ (most << b)}, device_id_type=MESH)
        copy.start()
        sends.append(copy)
        copy.wait_recv()

    for copy in got_r:
        copy.wait()
    got_leaf.wait()
    in_leaf.wait_recv()
    for k in range(rows // width):
        s = pl.ds(k * width, width)
        x[s] = r[s].astype(jnp.float32) + dot(leaf[s], rp[s])
    ready_v(top)
    narrow = tdot(v[top], x[...].astype(jnp.bfloat16)).astype(jnp.bfloat16)
    ready_u(top)
    x[...] = x[...] - dot(u[top], narrow)
    ready_v(top - 1)
    partial = tdot(v[top - 1], x[...].astype(jnp.bfloat16))

    for l in range(top - 1, -1, -1):
        group = 2 ** (top - l)
        h = min(group, most)
        pair = h == 2
        ch = rank if pair else rank // h
        j = me & (h - 1)
        mine = pl.ds(pl.multiple_of(j * ch, 16), ch)
        ps[l] = partial.astype(jnp.bfloat16)
        if pair:
            moved = [send(ps.at[l], rs.at[l], l, 0, 1)]
        else:
            moved = [
                send(ps.at[l, pl.ds(pl.multiple_of((j ^ o) * ch, 16), ch)],
                     rs.at[l, pl.ds((o - 1) * ch, ch)], l, 0, o)
                for o in range(h - 1, 0, -1)
            ]
            pf[...] = partial
        if l > 0:
            push_u(l - 1)
        if l > 1:
            push_v(l - 2)
        if l < top - 1:
            moved_x = x[...] - dot(u[l + 1], c[l + 1])
            x[...] = it[...].astype(jnp.float32) - moved_x if l == 0 else moved_x
        ready_u(l)
        if l == 1:
            got_it.wait()

        def ahead():
            ready_v(l - 1)
            term = tdot(v[l - 1], x[...].astype(jnp.bfloat16))
            cross = tdot(v[l - 1], u[l]).astype(jnp.bfloat16)
            return term, cross

        if pair:
            term, cross = ahead() if l > 0 else (None, None)
            for copy in moved:
                copy.wait_recv()
            c[l] = (partial + rs[l].astype(jnp.float32)).astype(jnp.bfloat16)
        else:
            for copy in moved:
                copy.wait_recv()
            total = pf[mine]
            for o in range(1, h):
                total = total + rs[l, pl.ds((o - 1) * ch, ch)].astype(jnp.float32)
            for b in range(log2(group // h)):
                xs[l, b] = total
                send_far(xs.at[l, b], xr.at[l, b], l, b)
                total = total + xr[l, b]
            c[l, mine] = total.astype(jnp.bfloat16)
            moved = [send(c.at[l, mine], c.at[l, mine], l, 1, o) for o in range(h - 1, 0, -1)]
            term, cross = ahead() if l > 0 else (None, None)
            for copy in moved:
                copy.wait_recv()
        if l > 0:
            partial = term - dot(cross, c[l])

    blocks = 4
    size = rows // blocks
    num = jnp.zeros((1, vecs), jnp.float32)
    den = jnp.zeros((1, vecs), jnp.float32)
    outs = []
    for k in range(blocks):
        s = pl.ds(k * size, size)
        updated = x[s] + dot(u[0, s], c[0])
        x[s] = updated
        copy = pltpu.make_async_copy(x.at[s], out_h.at[s], osem.at[k])
        copy.start()
        outs.append(copy)
        num = num + jnp.sum(updated * r[s].astype(jnp.float32), axis=0, keepdims=True)
        den = den + jnp.sum(updated * updated, axis=0, keepdims=True)
    st[pl.ds(0, 1)] = num
    st[pl.ds(1, 1)] = den
    moved = [send(st, sg.at[o - 1], top, 0, o) for o in range(most - 1, 0, -1)]
    for copy in moved:
        copy.wait_recv()
    total = st[...]
    for o in range(1, most):
        total = total + sg[o - 1]
    for b in range(log2(n // most)):
        sx[b] = total
        send_far(sx.at[b], sx.at[log2(n // most) + b], top, b)
        total = total + sx[log2(n // most) + b]
    fun_ref[...] = est_ref[...] + total[0:1] / (total[1:2] + epsilon)
    for copy in sends:
        copy.wait_send()
    for copy in outs:
        copy.wait()


def per_device(n, iterate, residual, leaf_offset, bases_v, bases_u, estimate):
    rows, vecs = residual.shape
    levels = bases_v.shape[0]
    rank = 2 * bases_v.shape[2]
    width = 2 * leaf_offset.shape[1]
    top = levels - 1
    most = min(n, MOST)
    far = max(log2(n // most), 1)
    hbm = pl.BlockSpec(memory_space=pl.ANY)
    vmem = pl.BlockSpec(memory_space=pltpu.VMEM)
    bf, f32 = jnp.bfloat16, jnp.float32
    updated, functional = pl.pallas_call(
        functools.partial(kernel, n),
        out_shape=(
            jax.ShapeDtypeStruct((rows, vecs), f32),
            jax.ShapeDtypeStruct((1, vecs), f32),
        ),
        in_specs=[hbm] * 5 + [vmem],
        out_specs=(hbm, vmem),
        scratch_shapes=[
            pltpu.VMEM((rows, vecs), bf),
            pltpu.VMEM((rows, vecs), bf),
            pltpu.VMEM((rows, vecs), bf),
            pltpu.VMEM((rows, width), bf),
            pltpu.VMEM((levels, rows, rank), bf),
            pltpu.VMEM((levels, rows, rank), bf),
            pltpu.VMEM((rows, vecs), f32),
            pltpu.VMEM((rank, vecs), f32),
            pltpu.VMEM((top, rank, vecs), bf),
            pltpu.VMEM((top, rank, vecs), bf),
            pltpu.VMEM((top, rank, vecs), bf),
            pltpu.VMEM((top, far, rank // most, vecs), f32),
            pltpu.VMEM((top, far, rank // most, vecs), f32),
            pltpu.VMEM((2, vecs), f32),
            pltpu.VMEM((most, 2, vecs), f32),
            pltpu.VMEM((2 * far, 2, vecs), f32),
            pltpu.SemaphoreType.DMA((2 * (rows // width) + 2 * levels + 3,)),
            pltpu.SemaphoreType.DMA((2 * levels + 1,)),
            pltpu.SemaphoreType.DMA((2 * levels + 1,)),
            pltpu.SemaphoreType.DMA((levels, 2, most)),
            pltpu.SemaphoreType.DMA((levels, 2, most)),
            pltpu.SemaphoreType.DMA((2, levels, far)),
            pltpu.SemaphoreType.DMA((4,)),
        ],
        compiler_params=pltpu.CompilerParams(
            collective_id=0, has_side_effects=True, vmem_limit_bytes=56 << 20
        ),
    )(iterate, residual, leaf_offset, bases_v, bases_u, estimate.reshape(1, vecs))
    return updated, functional.reshape(vecs)


def solution(mesh):
    return jax.shard_map(
        functools.partial(per_device, mesh.shape["rows"]),
        mesh=mesh,
        in_specs=(
            P("rows", "cols"),
            P("rows", "cols"),
            P("rows", "cols"),
            P(None, "rows", "cols"),
            P(None, "rows", "cols"),
            P("cols"),
        ),
        out_specs=(P("rows", "cols"), P("cols")),
        check_vma=False,
    )
```

```python
import functools

import jax
import jax.numpy as jnp
from jax import lax
from jax.experimental import pallas as pl
from jax.experimental.pallas import tpu as pltpu
from jax.sharding import PartitionSpec as P

epsilon = 1e-06
MESH = pl.DeviceIdType.MESH
MOST = 8


def log2(value):
    return value.bit_length() - 1


def tdot(a, b):
    return lax.dot_general(a, b, (((0,), (0,)), ((), ())), preferred_element_type=jnp.float32)


def dot(a, b):
    return jnp.dot(a, b, preferred_element_type=jnp.float32)


def kernel(n, it_h, r_h, leaf_h, v_h, u_h, est_ref, out_h, fun_ref,
           it, r, rp, leaf, v, u, x, pf, ps, rs, c, xs, xr, st, sg, sx,
           lsem, wsend, wrecv, ssem, rsem, xsem, osem):
    rows, vecs = r.shape
    rank = v.shape[2]
    half = rank // 2
    width = leaf.shape[1]
    lh = width // 2
    top = log2(n)
    most = min(n, MOST)
    me = lax.axis_index("rows")
    col = lax.axis_index("cols")
    other = 1 - col

    local = []

    def fetch(src, dst, slot):
        copy = pltpu.make_async_copy(src, dst, lsem.at[slot])
        copy.start()
        return copy

    base = 0
    got_r = []
    for k in range(rows // width):
        for part, which in enumerate((col, other)):
            start = pl.multiple_of(k * width + which * lh, 16)
            got_r.append(fetch(r_h.at[pl.ds(start, lh)], rp.at[pl.ds(k * width + part * lh, lh)], base))
            base += 1
    got_r.append(fetch(r_h, r, base))
    got_leaf = fetch(leaf_h, leaf.at[:, pl.ds(0, lh)], base + 1)
    base += 2

    barrier = pltpu.get_barrier_semaphore()
    pl.semaphore_signal(barrier, inc=1, device_id={"cols": other}, device_id_type=MESH)
    peers = list(range(1, most)) + [most << b for b in range(log2(n // most))]
    for o in peers:
        pl.semaphore_signal(barrier, inc=1, device_id={"rows": me ^ o}, device_id_type=MESH)
    pl.semaphore_wait(barrier, len(peers) + 1)

    sends = []

    def push(src, dst, slot):
        copy = pltpu.make_async_remote_copy(
            src_ref=src, dst_ref=dst, send_sem=wsend.at[slot], recv_sem=wrecv.at[slot],
            device_id={"cols": other}, device_id_type=MESH)
        copy.start()
        sends.append(copy)
        return copy

    in_leaf = push(leaf_h, leaf.at[:, pl.ds(lh, lh)], 0)
    in_v, in_u = {}, {}

    def push_v(l):
        in_v[l] = push(v_h.at[l], v.at[l, :, pl.ds(half, half)], 1 + 2 * l)

    def push_u(l):
        in_u[l] = push(u_h.at[l], u.at[l, :, pl.ds(half, half)], 2 + 2 * l)

    push_v(top)
    push_u(top)
    push_v(top - 1)
    push_u(top - 1)
    push_v(top - 2)

    got_v, got_u = {}, {}
    for l in range(top, -1, -1):
        got_v[l] = fetch(v_h.at[l], v.at[l, :, pl.ds(0, half)], base)
        got_u[l] = fetch(u_h.at[l], u.at[l, :, pl.ds(0, half)], base + 1)
        base += 2
    got_it = fetch(it_h, it, base)

    def ready_v(l):
        got_v[l].wait()
        in_v[l].wait_recv()

    def ready_u(l):
        got_u[l].wait()
        in_u[l].wait_recv()

    def send(src, dst, l, phase, o):
        copy = pltpu.make_async_remote_copy(
            src_ref=src, dst_ref=dst, send_sem=ssem.at[l, phase, o], recv_sem=rsem.at[l, phase, o],
            device_id={"rows": me ^ o}, device_id_type=MESH)
        copy.start()
        sends.append(copy)
        return copy

    def send_far(src, dst, l, b):
        copy = pltpu.make_async_remote_copy(
            src_ref=src, dst_ref=dst, send_sem=xsem.at[0, l, b], recv_sem=xsem.at[1, l, b],
            device_id={"rows": me ^ (most << b)}, device_id_type=MESH)
        copy.start()
        sends.append(copy)
        copy.wait_recv()

    for copy in got_r:
        copy.wait()
    got_leaf.wait()
    in_leaf.wait_recv()
    for k in range(rows // width):
        s = pl.ds(k * width, width)
        x[s] = r[s].astype(jnp.float32) + dot(leaf[s], rp[s])
    ready_v(top)
    narrow = tdot(v[top], x[...].astype(jnp.bfloat16)).astype(jnp.bfloat16)
    ready_u(top)
    x[...] = x[...] - dot(u[top], narrow)
    ready_v(top - 1)
    partial = tdot(v[top - 1], x[...].astype(jnp.bfloat16))

    for l in range(top - 1, -1, -1):
        group = 2 ** (top - l)
        h = min(group, most)
        pair = h == 2
        ch = rank if pair else rank // h
        j = me & (h - 1)
        mine = pl.ds(pl.multiple_of(j * ch, 16), ch)
        ps[l] = partial.astype(jnp.bfloat16)
        if pair:
            moved = [send(ps.at[l], rs.at[l], l, 0, 1)]
        else:
            moved = [
                send(ps.at[l, pl.ds(pl.multiple_of((j ^ o) * ch, 16), ch)],
                     rs.at[l, pl.ds((o - 1) * ch, ch)], l, 0, o)
                for o in range(h - 1, 0, -1)
            ]
            pf[...] = partial
        if l > 0:
            push_u(l - 1)
        if l > 1:
            push_v(l - 2)
        if l < top - 1:
            moved_x = x[...] - dot(u[l + 1], c[l + 1])
            x[...] = it[...].astype(jnp.float32) - moved_x if l == 0 else moved_x
        ready_u(l)
        if l == 1:
            got_it.wait()

        def ahead():
            ready_v(l - 1)
            term = tdot(v[l - 1], x[...].astype(jnp.bfloat16))
            cross = tdot(v[l - 1], u[l]).astype(jnp.bfloat16)
            return term, cross

        if pair:
            term, cross = ahead() if l > 0 else (None, None)
            for copy in moved:
                copy.wait_recv()
            c[l] = (partial + rs[l].astype(jnp.float32)).astype(jnp.bfloat16)
        else:
            for copy in moved:
                copy.wait_recv()
            total = pf[mine]
            for o in range(1, h):
                total = total + rs[l, pl.ds((o - 1) * ch, ch)].astype(jnp.float32)
            for b in range(log2(group // h)):
                xs[l, b] = total
                send_far(xs.at[l, b], xr.at[l, b], l, b)
                total = total + xr[l, b]
            c[l, mine] = total.astype(jnp.bfloat16)
            moved = [send(c.at[l, mine], c.at[l, mine], l, 1, o) for o in range(h - 1, 0, -1)]
            term, cross = ahead() if l > 0 else (None, None)
            for copy in moved:
                copy.wait_recv()
        if l > 0:
            partial = term - dot(cross, c[l])

    blocks = 4
    size = rows // blocks
    num = jnp.zeros((1, vecs), jnp.float32)
    den = jnp.zeros((1, vecs), jnp.float32)
    outs = []
    for k in range(blocks):
        s = pl.ds(k * size, size)
        updated = x[s] + dot(u[0, s], c[0])
        x[s] = updated
        copy = pltpu.make_async_copy(x.at[s], out_h.at[s], osem.at[k])
        copy.start()
        outs.append(copy)
        num = num + jnp.sum(updated * r[s].astype(jnp.float32), axis=0, keepdims=True)
        den = den + jnp.sum(updated * updated, axis=0, keepdims=True)
    st[pl.ds(0, 1)] = num
    st[pl.ds(1, 1)] = den
    moved = [send(st, sg.at[o - 1], top, 0, o) for o in range(most - 1, 0, -1)]
    for copy in moved:
        copy.wait_recv()
    total = st[...]
    for o in range(1, most):
        total = total + sg[o - 1]
    for b in range(log2(n // most)):
        sx[b] = total
        send_far(sx.at[b], sx.at[log2(n // most) + b], top, b)
        total = total + sx[log2(n // most) + b]
    fun_ref[...] = est_ref[...] + total[0:1] / (total[1:2] + epsilon)
    for copy in sends:
        copy.wait_send()
    for copy in outs:
        copy.wait()


def per_device(n, iterate, residual, leaf_offset, bases_v, bases_u, estimate):
    rows, vecs = residual.shape
    levels = bases_v.shape[0]
    rank = 2 * bases_v.shape[2]
    width = 2 * leaf_offset.shape[1]
    top = levels - 1
    most = min(n, MOST)
    far = max(log2(n // most), 1)
    hbm = pl.BlockSpec(memory_space=pl.ANY)
    vmem = pl.BlockSpec(memory_space=pltpu.VMEM)
    bf, f32 = jnp.bfloat16, jnp.float32
    updated, functional = pl.pallas_call(
        functools.partial(kernel, n),
        out_shape=(
            jax.ShapeDtypeStruct((rows, vecs), f32),
            jax.ShapeDtypeStruct((1, vecs), f32),
        ),
        in_specs=[hbm] * 5 + [vmem],
        out_specs=(hbm, vmem),
        scratch_shapes=[
            pltpu.VMEM((rows, vecs), bf),
            pltpu.VMEM((rows, vecs), bf),
            pltpu.VMEM((rows, vecs), bf),
            pltpu.VMEM((rows, width), bf),
            pltpu.VMEM((levels, rows, rank), bf),
            pltpu.VMEM((levels, rows, rank), bf),
            pltpu.VMEM((rows, vecs), f32),
            pltpu.VMEM((rank, vecs), f32),
            pltpu.VMEM((top, rank, vecs), bf),
            pltpu.VMEM((top, rank, vecs), bf),
            pltpu.VMEM((top, rank, vecs), bf),
            pltpu.VMEM((top, far, rank // most, vecs), f32),
            pltpu.VMEM((top, far, rank // most, vecs), f32),
            pltpu.VMEM((2, vecs), f32),
            pltpu.VMEM((most, 2, vecs), f32),
            pltpu.VMEM((2 * far, 2, vecs), f32),
            pltpu.SemaphoreType.DMA((2 * (rows // width) + 2 * levels + 3,)),
            pltpu.SemaphoreType.DMA((2 * levels + 1,)),
            pltpu.SemaphoreType.DMA((2 * levels + 1,)),
            pltpu.SemaphoreType.DMA((levels, 2, most)),
            pltpu.SemaphoreType.DMA((levels, 2, most)),
            pltpu.SemaphoreType.DMA((2, levels, far)),
            pltpu.SemaphoreType.DMA((4,)),
        ],
        compiler_params=pltpu.CompilerParams(
            collective_id=0, has_side_effects=True, vmem_limit_bytes=56 << 20
        ),
    )(iterate, residual, leaf_offset, bases_v, bases_u, estimate.reshape(1, vecs))
    return updated, functional.reshape(vecs)


def solution(mesh):
    return jax.shard_map(
        functools.partial(per_device, mesh.shape["rows"]),
        mesh=mesh,
        in_specs=(
            P("rows", "cols"),
            P("rows", "cols"),
            P("rows", "cols"),
            P(None, "rows", "cols"),
            P(None, "rows", "cols"),
            P("cols"),
        ),
        out_specs=(P("rows", "cols"), P("cols")),
        check_vma=False,
    )
```
